32 devices in a mesh: dp: 8 (over z, x), mp: 4 (over y, core).
Axes of the slice: x: 2, y: 2, z: 4, core: 2. Of those that a mesh axis runs over, the one named last changes fastest.
Arguments:
- activations: bfloat16 [4096, 3072], P('dp', 'mp'), may hold values from -6 to 6
- out_grads: bfloat16 [4096, 6144], P('dp', 'mp'), may hold values from -0.25 to 0.25
- error: bfloat16 [8, 3072, 6144], P('dp', 'mp'), may hold values from -8 to 8
- sketch: bfloat16 [6144, 64], replicated, may hold values from -0.078125 to 0.078125
- momentum: float32 [3072, 6144], P('mp', 'dp'), may hold values from -6 to 6
Outputs:
- error_new: bfloat16 [8, 3072, 6144], P('dp', 'mp')
- momentum_new: float32 [3072, 6144], P('mp', 'dp')
- next_sketch: bfloat16 [6144, 64], replicated
The draws below stay inside these ranges and needn't reach their ends.
All inputs are finite; a program needn't handle non-finite values.
Results may differ from the reference program's by a relative error of at most 0.0057.
Values may be sent and summed in bfloat16 or wider, within the bound.
A program may use at most 64 MiB of HBM per device.

```python
import jax
import jax.numpy as jnp
from jax import lax

D = 6144
ROWS = 3072
RANK = 64
TOK_DEV = 512
WORKERS = 8
TOKENS = 4096


def draw_error(key, part):
    shared = jax.random.normal(jax.random.fold_in(key, 11), (ROWS, D), jnp.float32)
    single = jax.random.normal(jax.random.fold_in(key, 12), (WORKERS, ROWS, D), jnp.float32)
    values = 0.8 * shared + 0.6 * single
    return jnp.clip(values, -8.0, 8.0).astype(jnp.bfloat16)


def steps_of(key, extent, pieces, smallest, largest):
    def one(axis_at, blocks):
        draws = jax.random.uniform(jax.random.fold_in(jax.random.fold_in(key, 6), axis_at), (blocks,), jnp.float32, smallest / len(pieces), largest / len(pieces))
        return jnp.repeat(jnp.exp(draws), extent[axis_at] // blocks).reshape((-1,) + (1,) * (len(extent) - axis_at - 1))

    gain = one(*pieces[0])
    for cut in pieces[1:]:
        gain = gain * one(*cut)
    return gain


def noise(rng, shape, spread, reach, shards=(), held_as=jnp.bfloat16):
    loudness = steps_of(rng, shape, shards, -0.22, 0.18) if shards else 1.0
    array = jax.random.normal(rng, shape, jnp.float32) * spread * loudness
    return jnp.minimum(jnp.maximum(array, -reach), reach).astype(held_as)


def setup_inputs(seed: int = 0) -> dict:
    seeds = jax.random.split(jax.random.key(seed), 6)
    return {
        "activations": noise(seeds[0], (TOKENS, ROWS), 1.0, 6.0, ((0, 8), (1, 4))),
        "out_grads": noise(seeds[1], (TOKENS, D), TOK_DEV ** -0.5, 0.25, ((0, 8), (1, 4))),
        "error": draw_error(jax.random.fold_in(seeds[5], 71), 0),
        "sketch": noise(seeds[3], (D, RANK), D ** -0.5, 0.078125),
        "momentum": noise(seeds[4], (ROWS, D), 1.0, 6.0, ((0, 4), (1, 8)), jnp.float32),
    }


beta_decay = 0.9

def reference(activations, out_grads, error, sketch, momentum):
    inputs = activations.reshape(WORKERS, TOK_DEV, ROWS)
    grads = out_grads.reshape(WORKERS, TOK_DEV, D)

    def feed_one(items):
        inputs_w, grads_w, error_w = items
        product = lax.dot_general(inputs_w.astype(jnp.float32), grads_w.astype(jnp.float32), (((0,), (0,)), ((), ())), preferred_element_type=jnp.float32)
        return (product + error_w.astype(jnp.float32)).astype(jnp.bfloat16)
    accumulated = lax.map(feed_one, (inputs, grads, error))

    def left_step(total, fed_w):
        return (total + jnp.dot(fed_w.astype(jnp.float32), sketch.astype(jnp.float32), preferred_element_type=jnp.float32), None)
    left_sketch = lax.scan(left_step, jnp.zeros((ROWS, RANK), jnp.float32), accumulated)[0]
    gram_matrix = jnp.dot(left_sketch.T.astype(jnp.float32), left_sketch.astype(jnp.float32), precision=lax.Precision.HIGHEST, preferred_element_type=jnp.float32)
    factor = jnp.linalg.cholesky(gram_matrix)
    basis_rows = jax.scipy.linalg.solve_triangular(factor, left_sketch.T, lower=True).T.astype(jnp.bfloat16)

    def right_step(total, fed_w):
        term = lax.dot_general(fed_w.astype(jnp.float32), basis_rows.astype(jnp.float32), (((0,), (0,)), ((), ())), preferred_element_type=jnp.float32)
        return (total + term, None)
    right_sketch = lax.scan(right_step, jnp.zeros((D, RANK), jnp.float32), accumulated)[0]
    next_sketch = right_sketch.astype(jnp.bfloat16)
    decoded = lax.dot_general(basis_rows.astype(jnp.float32), next_sketch.astype(jnp.float32), (((1,), (1,)), ((), ())), preferred_element_type=jnp.float32)
    momentum_new = beta_decay * momentum + decoded

    def error_one(fed_w):
        return (fed_w.astype(jnp.float32) - decoded / WORKERS).astype(jnp.bfloat16)
    error_new = lax.map(error_one, accumulated)
    return (error_new, momentum_new, next_sketch)
```

```python
import functools

import jax
import jax.numpy as jnp
from jax import lax
from jax.experimental import pallas as pl
from jax.experimental.pallas import tpu as pltpu
from jax.sharding import PartitionSpec as P

beta_decay = 0.9
F32, BF16 = jnp.float32, jnp.bfloat16
MESH = pl.DeviceIdType.MESH
HIGHEST = lax.Precision.HIGHEST


def native(activations, out_grads, error, sketch, momentum):
    product = lax.dot_general(
        activations,
        lax.all_gather(out_grads, "mp", axis=1, tiled=True),
        (((0,), (0,)), ((), ())),
        preferred_element_type=F32,
    )
    fed = (product + error[0].astype(F32)).astype(BF16)
    left = lax.psum(jnp.dot(fed, sketch, preferred_element_type=F32), "dp")
    gram = lax.psum(jnp.dot(left.T, left, precision=HIGHEST, preferred_element_type=F32), "mp")
    factor = jnp.linalg.cholesky(gram)
    basis = jax.scipy.linalg.solve_triangular(factor, left.T, lower=True).T.astype(BF16)
    right = lax.dot_general(fed, basis, (((0,), (0,)), ((), ())), preferred_element_type=F32)
    next_sketch = lax.psum(right, ("dp", "mp")).astype(BF16)
    width = momentum.shape[1]
    part = lax.dynamic_slice_in_dim(next_sketch, lax.axis_index("dp") * width, width, 0)
    momentum_new = beta_decay * momentum + lax.dot_general(
        basis, part, (((1,), (1,)), ((), ())), preferred_element_type=F32
    )
    decoded = lax.dot_general(
        basis, next_sketch, (((1,), (1,)), ((), ())), preferred_element_type=F32
    )
    error_new = (fed.astype(F32) - decoded / lax.axis_size("dp")).astype(BF16)
    return (error_new[None], momentum_new, next_sketch)


class Exchange:
    def __init__(self, axis, count, me, source, target, send_sem, recv_sem):
        self.axis, self.count, self.me = axis, count, me
        self.source, self.target = source, target
        self.send_sem, self.recv_sem = send_sem, recv_sem

    def copy(self, step, sender):
        peer = lax.rem(self.me + step, self.count)
        slot = self.me if sender else peer
        return pltpu.make_async_remote_copy(
            src_ref=self.source(peer),
            dst_ref=self.target(slot),
            send_sem=self.send_sem.at[step],
            recv_sem=self.recv_sem.at[slot],
            device_id={self.axis: peer},
            device_id_type=MESH,
        )

    def start(self):
        for step in range(1, self.count):
            self.copy(step, True).start()
        return self

    def wait(self):
        for step in range(1, self.count):
            self.copy(step, False).wait_recv()
        for step in range(1, self.count):
            self.copy(step, True).wait_send()


def total(slots, count):
    result = slots[0].astype(F32)
    for index in range(1, count):
        result = result + slots[index].astype(F32)
    return result


def inverse_factor(gram):
    rank = gram.shape[0]
    rows = lax.broadcasted_iota(jnp.int32, (rank, rank), 0)
    columns = lax.broadcasted_iota(jnp.int32, (rank, rank), 1)
    unit = (rows == columns).astype(F32)
    both = jnp.concatenate([gram, unit], axis=1)
    below = lax.broadcasted_iota(jnp.int32, (rank, 1), 0)
    for k in range(rank - 1):
        row = both[k : k + 1, :]
        scaled = row * (1.0 / row[:, k : k + 1])
        column = jnp.where(below > k, both[:, k : k + 1], 0.0)
        both = both - column * scaled
    pivots = jnp.sum(both[:, :rank] * unit, axis=1, keepdims=True)
    return both[:, rank:] * (1.0 / jnp.sqrt(pivots))


def chain_kernel(
    dp, mp, a_ref, g_ref, s_ref, e_hbm, basis_ref, sketch_ref,
    e_ref, gs, lf, lr, la, gm, ht, rt, rb, rr, qb, qr, nm,
    e_sem, mp_send, mp_recv, dp_send, dp_recv,
):
    me_d, me_m = lax.axis_index("dp"), lax.axis_index("mp")
    rows, width = e_ref.shape
    rank = s_ref.shape[1]
    columns = g_ref.shape[1]
    slab = rows // dp
    band = rank // mp
    block = width // dp

    def load(index):
        part = pl.ds(pl.multiple_of(index * slab, slab), slab)
        return pltpu.make_async_copy(e_hbm.at[0, part], e_ref.at[part], e_sem.at[index])

    for index in range(dp):
        load(index).start()

    barrier = pltpu.get_barrier_semaphore()
    for step in range(1, mp):
        pl.semaphore_signal(
            barrier, inc=1, device_id={"mp": lax.rem(me_m + step, mp)}, device_id_type=MESH
        )
    for step in range(1, dp):
        pl.semaphore_signal(
            barrier, inc=1, device_id={"dp": lax.rem(me_d + step, dp)}, device_id_type=MESH
        )
    pl.semaphore_wait(barrier, mp + dp - 2)

    mine = pl.ds(pl.multiple_of(me_m * columns, columns), columns)
    gs[me_m] = jnp.dot(g_ref[...], s_ref[mine, :], preferred_element_type=F32).T.astype(BF16)
    share = Exchange(
        "mp", mp, me_m, lambda p: gs.at[me_m], lambda p: gs.at[p], mp_send.at[0], mp_recv.at[0]
    ).start()

    def sketch_slab(index, carry):
        load(index).wait()
        part = pl.ds(pl.multiple_of(index * slab, slab), slab)
        lf[index] = jnp.dot(e_ref[part, :], s_ref[...], preferred_element_type=F32)
        return carry

    lax.fori_loop(0, dp, sketch_slab, 0)
    share.wait()
    grad_left = jnp.dot(total(gs, mp).astype(BF16), a_ref[...], preferred_element_type=F32).T
    lf[...] = lf[...] + grad_left.reshape(dp, slab, rank)

    share = Exchange(
        "dp", dp, me_d, lambda p: lf.at[p], lambda p: lr.at[p], dp_send.at[0], dp_recv.at[0]
    ).start()
    lr[me_d] = lf[me_d]
    share.wait()
    la[me_d] = total(lr, dp)
    share = Exchange(
        "dp", dp, me_d, lambda p: la.at[me_d], lambda p: la.at[p], dp_send.at[1], dp_recv.at[1]
    ).start()
    share.wait()
    left = la[...].reshape(rows, rank)
    gm[me_m] = jnp.dot(left.T, left, precision=HIGHEST, preferred_element_type=F32)
    share = Exchange(
        "mp", mp, me_m, lambda p: gm.at[me_m], lambda p: gm.at[p], mp_send.at[1], mp_recv.at[1]
    ).start()
    share.wait()
    inverse = inverse_factor(total(gm, mp))
    basis = jnp.dot(left, inverse.T, precision=HIGHEST, preferred_element_type=F32)
    basis_ref[...] = basis.astype(BF16)
    basis_t = basis.T.astype(BF16)

    ht[me_m] = jnp.dot(a_ref[...], basis_ref[...], preferred_element_type=F32).T.astype(BF16)
    share = Exchange(
        "mp", mp, me_m, lambda p: ht.at[me_m], lambda p: ht.at[p], mp_send.at[2], mp_recv.at[2]
    ).start()

    def right_block(index, carry):
        part = pl.ds(pl.multiple_of(index * block, block), block)
        rt[:, part] = jnp.dot(basis_t, e_ref[:, part], preferred_element_type=F32)
        return carry

    lax.fori_loop(0, dp, right_block, 0)
    share.wait()
    rt[:, mine] = rt[:, mine] + jnp.dot(
        total(ht, mp).astype(BF16), g_ref[...], preferred_element_type=F32
    )

    for index in range(mp):
        rb[index] = rt[index * band : (index + 1) * band, :].astype(BF16)
    share = Exchange(
        "mp", mp, me_m, lambda p: rb.at[p], lambda p: rr.at[p], mp_send.at[3], mp_recv.at[3]
    ).start()
    rr[me_m] = rb[me_m]
    share.wait()
    band_sum = total(rr, mp).astype(BF16)
    for index in range(dp):
        qb[index] = band_sum[:, index * block : (index + 1) * block]
    share = Exchange(
        "dp", dp, me_d, lambda p: qb.at[p], lambda p: qr.at[p], dp_send.at[2], dp_recv.at[2]
    ).start()
    qr[me_d] = qb[me_d]
    share.wait()
    nm[me_m, me_d] = total(qr, dp).astype(BF16)
    share = Exchange(
        "dp", dp, me_d, lambda p: nm.at[me_m, me_d], lambda p: nm.at[me_m, p],
        dp_send.at[3], dp_recv.at[3],
    ).start()
    share.wait()
    share = Exchange(
        "mp", mp, me_m, lambda p: nm.at[me_m], lambda p: nm.at[p], mp_send.at[4], mp_recv.at[4]
    ).start()
    share.wait()
    for m in range(mp):
        for d in range(dp):
            sketch_ref[m * band : (m + 1) * band, d * block : (d + 1) * block] = nm[m, d]


def finish_kernel(dp, a_ref, g_ref, e_ref, n_ref, b_ref, m_ref, error_ref, momentum_ref, turned):
    index = pl.program_id(0)

    @pl.when(index == 0)
    def _():
        turned[...] = a_ref[...].T

    product = jnp.dot(turned[...], g_ref[...], preferred_element_type=F32)
    fed = (product + e_ref[0].astype(F32)).astype(BF16)
    decoded = jnp.dot(b_ref[...], n_ref[...], preferred_element_type=F32)
    error_ref[0] = (fed.astype(F32) - decoded / dp).astype(BF16)

    @pl.when(index == lax.axis_index("dp"))
    def _():
        momentum_ref[...] = beta_decay * m_ref[...] + decoded


def step(dp, mp, activations, out_grads, error, sketch, momentum):
    tokens, rows = activations.shape
    columns = out_grads.shape[1]
    width, rank = sketch.shape
    block = momentum.shape[1]
    if rows % (16 * dp) or rank % (16 * mp) or block % 128 or columns % 128:
        return native(activations, out_grads, error, sketch, momentum)
    slab, band = rows // dp, rank // mp
    gathered = lax.all_gather(out_grads, "mp", axis=1, tiled=True)
    vmem = pl.BlockSpec(memory_space=pltpu.VMEM)
    basis, sketch_t = pl.pallas_call(
        functools.partial(chain_kernel, dp, mp),
        out_shape=(
            jax.ShapeDtypeStruct((rows, rank), BF16),
            jax.ShapeDtypeStruct((rank, width), BF16),
        ),
        in_specs=[vmem, vmem, vmem, pl.BlockSpec(memory_space=pl.ANY)],
        out_specs=(vmem, vmem),
        scratch_shapes=[
            pltpu.VMEM((rows, width), BF16),
            pltpu.VMEM((mp, rank, tokens), BF16),
            pltpu.VMEM((dp, slab, rank), F32),
            pltpu.VMEM((dp, slab, rank), F32),
            pltpu.VMEM((dp, slab, rank), F32),
            pltpu.VMEM((mp, rank, rank), F32),
            pltpu.VMEM((mp, rank, tokens), BF16),
            pltpu.VMEM((rank, width), F32),
            pltpu.VMEM((mp, band, width), BF16),
            pltpu.VMEM((mp, band, width), BF16),
            pltpu.VMEM((dp, band, block), BF16),
            pltpu.VMEM((dp, band, block), BF16),
            pltpu.VMEM((mp, dp, band, block), BF16),
            pltpu.SemaphoreType.DMA((dp,)),
            pltpu.SemaphoreType.DMA((5, mp)),
            pltpu.SemaphoreType.DMA((5, mp)),
            pltpu.SemaphoreType.DMA((4, dp)),
            pltpu.SemaphoreType.DMA((4, dp)),
        ],
        compiler_params=pltpu.CompilerParams(
            collective_id=0, has_side_effects=True, vmem_limit_bytes=56 << 20
        ),
        cost_estimate=pl.CostEstimate(
            flops=4 * rows * width * rank, bytes_accessed=8 * rows * width, transcendentals=0
        ),
        name="chain",
    )(activations, out_grads, sketch, error)
    whole = lambda shape: pl.BlockSpec(shape, lambda i: (0,) * len(shape))
    error_new, momentum_new = pl.pallas_call(
        functools.partial(finish_kernel, dp),
        grid=(dp,),
        out_shape=(
            jax.ShapeDtypeStruct(error.shape, BF16),
            jax.ShapeDtypeStruct(momentum.shape, F32),
        ),
        in_specs=[
            whole((tokens, rows)),
            pl.BlockSpec((tokens, block), lambda i: (0, i)),
            pl.BlockSpec((1, rows, block), lambda i: (0, 0, i)),
            pl.BlockSpec((rank, block), lambda i: (0, i)),
            whole((rows, rank)),
            whole((rows, block)),
        ],
        out_specs=(
            pl.BlockSpec((1, rows, block), lambda i: (0, 0, i)),
            whole((rows, block)),
        ),
        scratch_shapes=[pltpu.VMEM((rows, tokens), BF16)],
        compiler_params=pltpu.CompilerParams(
            dimension_semantics=("arbitrary",), vmem_limit_bytes=56 << 20
        ),
        name="finish",
    )(activations, gathered, error, sketch_t, basis, momentum)
    return (error_new, momentum_new, sketch_t.T)


def solution(mesh):
    body = functools.partial(step, mesh.shape["dp"], mesh.shape["mp"])
    in_specs = (P("dp", "mp"), P("dp", "mp"), P("dp", "mp", None), P(), P("mp", "dp"))
    out_specs = (P("dp", "mp", None), P("mp", "dp"), P())
    return jax.shard_map(body, mesh=mesh, in_specs=in_specs, out_specs=out_specs, check_vma=False)
```

```python
import functools

import jax
import jax.numpy as jnp
from jax import lax
from jax.experimental import pallas as pl
from jax.experimental.pallas import tpu as pltpu
from jax.sharding import PartitionSpec as P

beta_decay = 0.9
F32, BF16 = jnp.float32, jnp.bfloat16
MESH = pl.DeviceIdType.MESH
HIGHEST = lax.Precision.HIGHEST


def native(activations, out_grads, error, sketch, momentum):
    product = lax.dot_general(
        activations,
        lax.all_gather(out_grads, "mp", axis=1, tiled=True),
        (((0,), (0,)), ((), ())),
        preferred_element_type=F32,
    )
    fed = (product + error[0].astype(F32)).astype(BF16)
    left = lax.psum(jnp.dot(fed, sketch, preferred_element_type=F32), "dp")
    gram = lax.psum(jnp.dot(left.T, left, precision=HIGHEST, preferred_element_type=F32), "mp")
    factor = jnp.linalg.cholesky(gram)
    basis = jax.scipy.linalg.solve_triangular(factor, left.T, lower=True).T.astype(BF16)
    right = lax.dot_general(fed, basis, (((0,), (0,)), ((), ())), preferred_element_type=F32)
    next_sketch = lax.psum(right, ("dp", "mp")).astype(BF16)
    width = momentum.shape[1]
    part = lax.dynamic_slice_in_dim(next_sketch, lax.axis_index("dp") * width, width, 0)
    momentum_new = beta_decay * momentum + lax.dot_general(
        basis, part, (((1,), (1,)), ((), ())), preferred_element_type=F32
    )
    decoded = lax.dot_general(
        basis, next_sketch, (((1,), (1,)), ((), ())), preferred_element_type=F32
    )
    error_new = (fed.astype(F32) - decoded / lax.axis_size("dp")).astype(BF16)
    return (error_new[None], momentum_new, next_sketch)


class Exchange:
    def __init__(self, axis, count, me, source, target, send_sem, recv_sem):
        self.axis, self.count, self.me = axis, count, me
        self.source, self.target = source, target
        self.send_sem, self.recv_sem = send_sem, recv_sem

    def place(self, peer):
        return peer

    def copy(self, step, sender):
        peer = lax.rem(self.me + step, self.count)
        slot = self.me if sender else peer
        return pltpu.make_async_remote_copy(
            src_ref=self.source(peer),
            dst_ref=self.target(slot),
            send_sem=self.send_sem.at[step],
            recv_sem=self.recv_sem.at[slot],
            device_id={self.axis: self.place(peer)},
            device_id_type=MESH,
        )

    def start(self):
        for step in range(1, self.count):
            self.copy(step, True).start()
        return self

    def wait_recv(self):
        for step in range(1, self.count):
            self.copy(step, False).wait_recv()

    def wait_send(self):
        for step in range(1, self.count):
            self.copy(step, True).wait_send()

    def wait(self):
        self.wait_recv()
        self.wait_send()


class Far(Exchange):
    def __init__(self, chips, chip, core, source, target, send_sem, recv_sem):
        super().__init__("mp", chips, chip, source, target, send_sem, recv_sem)
        self.core = core

    def place(self, peer):
        return 2 * peer + self.core


def total(slots, count):
    result = slots[0].astype(F32)
    for index in range(1, count):
        result = result + slots[index].astype(F32)
    return result


def inverse_factor(gram):
    rank = gram.shape[0]
    rows = lax.broadcasted_iota(jnp.int32, (rank, rank), 0)
    columns = lax.broadcasted_iota(jnp.int32, (rank, rank), 1)
    unit = (rows == columns).astype(F32)
    both = jnp.concatenate([gram, unit], axis=1)
    below = lax.broadcasted_iota(jnp.int32, (rank, 1), 0)
    for k in range(rank - 1):
        row = both[k : k + 1, :]
        scaled = row * (1.0 / row[:, k : k + 1])
        column = jnp.where(below > k, both[:, k : k + 1], 0.0)
        both = both - column * scaled
    pivots = jnp.sum(both[:, :rank] * unit, axis=1, keepdims=True)
    return both[:, rank:] * (1.0 / jnp.sqrt(pivots))


def chain_kernel(
    dp, mp, a_ref, g_ref, st_ref, e_hbm, basis_ref, sketch_ref,
    e_ref, s_ref, es, gs, lf, lr, la, gm, ht, rt, rb, rc, rd, ro, qb, qr, nm,
    e_sem, mp_send, mp_recv, dp_send, dp_recv, pair_send, pair_recv, far_send, far_recv,
):
    me_d, me_m = lax.axis_index("dp"), lax.axis_index("mp")
    rows, width = e_ref.shape
    rank = st_ref.shape[0]
    columns = g_ref.shape[1]
    slab = rows // dp
    band = rank // mp
    block = width // dp

    def load(index):
        part = pl.ds(pl.multiple_of(index * slab, slab), slab)
        return pltpu.make_async_copy(e_hbm.at[0, part], e_ref.at[part], e_sem.at[index])

    for index in range(dp):
        load(index).start()

    barrier = pltpu.get_barrier_semaphore()
    for step in range(1, mp):
        pl.semaphore_signal(
            barrier, inc=1, device_id={"mp": lax.rem(me_m + step, mp)}, device_id_type=MESH
        )
    for step in range(1, dp):
        pl.semaphore_signal(
            barrier, inc=1, device_id={"dp": lax.rem(me_d + step, dp)}, device_id_type=MESH
        )
    pl.semaphore_wait(barrier, mp + dp - 2)

    s_ref[...] = st_ref[...].T

    mine = pl.ds(pl.multiple_of(me_m * columns, columns), columns)
    gs[me_m] = jnp.dot(g_ref[...], s_ref[mine, :], preferred_element_type=F32).T.astype(BF16)
    share = Exchange(
        "mp", mp, me_m, lambda p: gs.at[me_m], lambda p: gs.at[p], mp_send.at[0], mp_recv.at[0]
    ).start()

    def sketch_slab(index, carry):
        load(index).wait()
        part = pl.ds(pl.multiple_of(index * slab, slab), slab)
        es[part, :] = jnp.dot(e_ref[part, :], s_ref[...], preferred_element_type=F32)
        return carry

    lax.fori_loop(0, dp, sketch_slab, 0)
    share.wait()
    grad_left = jnp.dot(total(gs, mp).astype(BF16), a_ref[...], preferred_element_type=F32).T
    local_left = es[...] + grad_left
    half = slab // 2
    for index in range(dp):
        top = local_left[index * slab : index * slab + half]
        low = local_left[index * slab + half : (index + 1) * slab]
        lf[index] = jnp.concatenate([top, low], axis=1)

    share = Exchange(
        "dp", dp, me_d, lambda p: lf.at[p], lambda p: lr.at[p], dp_send.at[0], dp_recv.at[0]
    ).start()
    lr[me_d] = lf[me_d]
    share.wait()
    la[me_d] = total(lr, dp)
    share = Exchange(
        "dp", dp, me_d, lambda p: la.at[me_d], lambda p: la.at[p], dp_send.at[1], dp_recv.at[1]
    ).start()
    share.wait()
    left = jnp.concatenate(
        [la[i][:, j * rank : (j + 1) * rank] for i in range(dp) for j in range(2)], axis=0
    )
    gm[me_m] = jnp.dot(left.T, left, precision=HIGHEST, preferred_element_type=F32)
    share = Exchange(
        "mp", mp, me_m, lambda p: gm.at[me_m], lambda p: gm.at[p], mp_send.at[1], mp_recv.at[1]
    ).start()
    share.wait()
    inverse = inverse_factor(total(gm, mp))
    basis = jnp.dot(left, inverse.T, precision=HIGHEST, preferred_element_type=F32)
    basis_ref[...] = basis.astype(BF16)
    basis_t = basis.T.astype(BF16)

    ht[me_m] = jnp.dot(a_ref[...], basis_ref[...], preferred_element_type=F32).T.astype(BF16)
    share = Exchange(
        "mp", mp, me_m, lambda p: ht.at[me_m], lambda p: ht.at[p], mp_send.at[2], mp_recv.at[2]
    ).start()

    def right_block(index, carry):
        part = pl.ds(pl.multiple_of(index * block, block), block)
        rt[:, part] = jnp.dot(basis_t, e_ref[:, part], preferred_element_type=F32)
        return carry

    lax.fori_loop(0, dp, right_block, 0)
    share.wait()
    rt[:, mine] = rt[:, mine] + jnp.dot(
        total(ht, mp).astype(BF16), g_ref[...], preferred_element_type=F32
    )

    core, chip, chips = lax.rem(me_m, 2), me_m // 2, mp // 2
    partner = me_m + 1 - 2 * core

    def pair_copy(sem, d, source, target):
        return pltpu.make_async_remote_copy(
            src_ref=source,
            dst_ref=target,
            send_sem=pair_send.at[sem, d],
            recv_sem=pair_recv.at[sem, d],
            device_id={"mp": partner},
            device_id_type=MESH,
        )

    def far(sem, d, source, target):
        return Far(chips, chip, core, source, target, far_send.at[sem, d], far_recv.at[sem, d])

    pairs, fars = [], []
    for d in range(dp):
        for m in range(mp):
            rb[d, m % 2, m // 2] = rt[
                m * band : (m + 1) * band, d * block : (d + 1) * block
            ].astype(BF16)
        pairs.append(pair_copy(0, d, rb.at[d, 1 - core], rc.at[d]))
        pairs[-1].start()
    for d in range(dp):
        pairs[d].wait_recv()
        rd[d] = (rb[d, core].astype(F32) + rc[d].astype(F32)).astype(BF16)
        fars.append(far(0, d, lambda p, d=d: rd.at[d, p], lambda p, d=d: ro.at[d, p]))
        fars[-1].start()
        ro[d, chip] = rd[d, chip]
    for d in range(dp):
        fars[d].wait_recv()
        qb[d] = total(ro.at[d], chips).astype(BF16)

        @pl.when(me_d != d)
        def _():
            pltpu.make_async_remote_copy(
                src_ref=qb.at[d],
                dst_ref=qr.at[me_d],
                send_sem=dp_send.at[2, d],
                recv_sem=dp_recv.at[2, me_d],
                device_id={"dp": d},
                device_id_type=MESH,
            ).start()

    for each in pairs + fars:
        each.wait_send()
    qr[me_d] = qb[me_d]
    for step in range(1, dp):
        peer = lax.rem(me_d + step, dp)
        pltpu.make_async_remote_copy(
            src_ref=qb.at[peer],
            dst_ref=qr.at[peer],
            send_sem=dp_send.at[2, peer],
            recv_sem=dp_recv.at[2, peer],
            device_id={"dp": peer},
            device_id_type=MESH,
        ).wait()

    nm[me_m, me_d] = total(qr, dp).astype(BF16)
    share = Exchange(
        "dp", dp, me_d, lambda p: nm.at[me_m, me_d], lambda p: nm.at[me_m, p],
        dp_send.at[3], dp_recv.at[3],
    ).start()
    pairs, fars = [], []
    for step in range(dp):
        d = lax.rem(me_d + step, dp)
        if step:
            share.copy(step, False).wait_recv()
        fars.append(
            far(
                1, step,
                lambda p, d=d: nm.at[me_m, d],
                lambda p, d=d: nm.at[2 * p + core, d],
            ).start()
        )
        pairs.append(pair_copy(1, step, nm.at[me_m, d], nm.at[me_m, d]))
        pairs[-1].start()
    relays = []
    for step in range(dp):
        d = lax.rem(me_d + step, dp)
        for hop in range(1, chips):
            fars[step].copy(hop, False).wait_recv()
            slot = 2 * lax.rem(chip + hop, chips) + core
            relays.append(pair_copy(1 + hop, step, nm.at[slot, d], nm.at[slot, d]))
            relays[-1].start()
    for copy in pairs + relays:
        copy.wait()
    for each in fars:
        each.wait_send()
    share.wait_send()
    for m in range(mp):
        for d in range(dp):
            sketch_ref[m * band : (m + 1) * band, d * block : (d + 1) * block] = nm[m, d]


def finish_kernel(dp, a_ref, g_ref, e_ref, n_ref, b_ref, m_ref, error_ref, momentum_ref, turned):
    index = pl.program_id(0)

    @pl.when(index == 0)
    def _():
        turned[...] = a_ref[...].T

    product = jnp.dot(turned[...], g_ref[...], preferred_element_type=F32)
    fed = (product + e_ref[0].astype(F32)).astype(BF16)
    decoded = jnp.dot(b_ref[...], n_ref[...], preferred_element_type=F32)
    error_ref[0] = (fed.astype(F32) - decoded / dp).astype(BF16)

    @pl.when(index == lax.axis_index("dp"))
    def _():
        momentum_ref[...] = beta_decay * m_ref[...] + decoded


def step(dp, mp, activations, out_grads, error, sketch, momentum):
    tokens, rows = activations.shape
    columns = out_grads.shape[1]
    width, rank = sketch.shape
    block = momentum.shape[1]
    if rows % (16 * dp) or rank % (16 * mp) or block % 128 or columns % 128 or mp % 2:
        return native(activations, out_grads, error, sketch, momentum)
    slab, band = rows // dp, rank // mp
    gathered = lax.all_gather(out_grads, "mp", axis=1, tiled=True)
    vmem = pl.BlockSpec(memory_space=pltpu.VMEM)
    basis, sketch_t = pl.pallas_call(
        functools.partial(chain_kernel, dp, mp),
        out_shape=(
            jax.ShapeDtypeStruct((rows, rank), BF16),
            jax.ShapeDtypeStruct((rank, width), BF16),
        ),
        in_specs=[vmem, vmem, vmem, pl.BlockSpec(memory_space=pl.ANY)],
        out_specs=(vmem, vmem),
        scratch_shapes=[
            pltpu.VMEM((rows, width), BF16),
            pltpu.VMEM((width, rank), BF16),
            pltpu.VMEM((rows, rank), F32),
            pltpu.VMEM((mp, rank, tokens), BF16),
            pltpu.VMEM((dp, slab // 2, 2 * rank), F32),
            pltpu.VMEM((dp, slab // 2, 2 * rank), F32),
            pltpu.VMEM((dp, slab // 2, 2 * rank), F32),
            pltpu.VMEM((mp, rank, rank), F32),
            pltpu.VMEM((mp, rank, tokens), BF16),
            pltpu.VMEM((rank, width), F32),
            pltpu.VMEM((dp, 2, mp // 2, band, block), BF16),
            pltpu.VMEM((dp, mp // 2, band, block), BF16),
            pltpu.VMEM((dp, mp // 2, band, block), BF16),
            pltpu.VMEM((dp, mp // 2, band, block), BF16),
            pltpu.VMEM((dp, band, block), BF16),
            pltpu.VMEM((dp, band, block), BF16),
            pltpu.VMEM((mp, dp, band, block), BF16),
            pltpu.SemaphoreType.DMA((dp,)),
            pltpu.SemaphoreType.DMA((5, mp)),
            pltpu.SemaphoreType.DMA((5, mp)),
            pltpu.SemaphoreType.DMA((4, dp)),
            pltpu.SemaphoreType.DMA((4, dp)),
            pltpu.SemaphoreType.DMA((1 + mp // 2, dp)),
            pltpu.SemaphoreType.DMA((1 + mp // 2, dp)),
            pltpu.SemaphoreType.DMA((2, dp, mp // 2)),
            pltpu.SemaphoreType.DMA((2, dp, mp // 2)),
        ],
        compiler_params=pltpu.CompilerParams(
            collective_id=0, has_side_effects=True, vmem_limit_bytes=56 << 20
        ),
        cost_estimate=pl.CostEstimate(
            flops=4 * rows * width * rank, bytes_accessed=8 * rows * width, transcendentals=0
        ),
        name="chain",
    )(activations, out_grads, sketch.T, error)
    whole = lambda shape: pl.BlockSpec(shape, lambda i: (0,) * len(shape))
    error_new, momentum_new = pl.pallas_call(
        functools.partial(finish_kernel, dp),
        grid=(dp,),
        out_shape=(
            jax.ShapeDtypeStruct(error.shape, BF16),
            jax.ShapeDtypeStruct(momentum.shape, F32),
        ),
        in_specs=[
            whole((tokens, rows)),
            pl.BlockSpec((tokens, block), lambda i: (0, i)),
            pl.BlockSpec((1, rows, block), lambda i: (0, 0, i)),
            pl.BlockSpec((rank, block), lambda i: (0, i)),
            whole((rows, rank)),
            whole((rows, block)),
        ],
        out_specs=(
            pl.BlockSpec((1, rows, block), lambda i: (0, 0, i)),
            whole((rows, block)),
        ),
        scratch_shapes=[pltpu.VMEM((rows, tokens), BF16)],
        compiler_params=pltpu.CompilerParams(
            dimension_semantics=("arbitrary",), vmem_limit_bytes=56 << 20
        ),
        name="finish",
    )(activations, gathered, error, sketch_t, basis, momentum)
    return (error_new, momentum_new, sketch_t.T)


def solution(mesh):
    body = functools.partial(step, mesh.shape["dp"], mesh.shape["mp"])
    in_specs = (P("dp", "mp"), P("dp", "mp"), P("dp", "mp", None), P(), P("mp", "dp"))
    out_specs = (P("dp", "mp", None), P("mp", "dp"), P())
    return jax.shard_map(body, mesh=mesh, in_specs=in_specs, out_specs=out_specs, check_vma=False)
```

```python
import functools

import jax
import jax.numpy as jnp
from jax import lax
from jax.experimental import pallas as pl
from jax.experimental.pallas import tpu as pltpu
from jax.sharding import PartitionSpec as P

beta_decay = 0.9
CHUNKS = 8
F32, BF16 = jnp.float32, jnp.bfloat16
MESH = pl.DeviceIdType.MESH
HIGHEST = lax.Precision.HIGHEST


def native(activations, out_grads, error, sketch, momentum):
    product = lax.dot_general(
        activations,
        lax.all_gather(out_grads, "mp", axis=1, tiled=True),
        (((0,), (0,)), ((), ())),
        preferred_element_type=F32,
    )
    fed = (product + error[0].astype(F32)).astype(BF16)
    left = lax.psum(jnp.dot(fed, sketch, preferred_element_type=F32), "dp")
    gram = lax.psum(jnp.dot(left.T, left, precision=HIGHEST, preferred_element_type=F32), "mp")
    factor = jnp.linalg.cholesky(gram)
    basis = jax.scipy.linalg.solve_triangular(factor, left.T, lower=True).T.astype(BF16)
    right = lax.dot_general(fed, basis, (((0,), (0,)), ((), ())), preferred_element_type=F32)
    next_sketch = lax.psum(right, ("dp", "mp")).astype(BF16)
    width = momentum.shape[1]
    part = lax.dynamic_slice_in_dim(next_sketch, lax.axis_index("dp") * width, width, 0)
    momentum_new = beta_decay * momentum + lax.dot_general(
        basis, part, (((1,), (1,)), ((), ())), preferred_element_type=F32
    )
    decoded = lax.dot_general(
        basis, next_sketch, (((1,), (1,)), ((), ())), preferred_element_type=F32
    )
    error_new = (fed.astype(F32) - decoded / lax.axis_size("dp")).astype(BF16)
    return (error_new[None], momentum_new, next_sketch)


class Exchange:
    def __init__(self, axis, count, me, source, target, send_sem, recv_sem):
        self.axis, self.count, self.me = axis, count, me
        self.source, self.target = source, target
        self.send_sem, self.recv_sem = send_sem, recv_sem

    def place(self, peer):
        return peer

    def copy(self, step, sender):
        peer = lax.rem(self.me + step, self.count)
        slot = self.me if sender else peer
        return pltpu.make_async_remote_copy(
            src_ref=self.source(peer),
            dst_ref=self.target(slot),
            send_sem=self.send_sem.at[step],
            recv_sem=self.recv_sem.at[slot],
            device_id={self.axis: self.place(peer)},
            device_id_type=MESH,
        )

    def start(self):
        for step in range(1, self.count):
            self.copy(step, True).start()
        return self

    def wait_recv(self):
        for step in range(1, self.count):
            self.copy(step, False).wait_recv()

    def wait_send(self):
        for step in range(1, self.count):
            self.copy(step, True).wait_send()

    def wait(self):
        self.wait_recv()
        self.wait_send()


class Far(Exchange):
    def __init__(self, chips, chip, core, source, target, send_sem, recv_sem):
        super().__init__("mp", chips, chip, source, target, send_sem, recv_sem)
        self.core = core

    def place(self, peer):
        return 2 * peer + self.core


def total(slots, count):
    result = slots[0].astype(F32)
    for index in range(1, count):
        result = result + slots[index].astype(F32)
    return result


def inverse_factor(gram):
    rank = gram.shape[0]
    rows = lax.broadcasted_iota(jnp.int32, (rank, rank), 0)
    columns = lax.broadcasted_iota(jnp.int32, (rank, rank), 1)
    unit = (rows == columns).astype(F32)
    both = jnp.concatenate([gram, unit], axis=1)
    below = lax.broadcasted_iota(jnp.int32, (rank, 1), 0)
    for k in range(rank - 1):
        row = both[k : k + 1, :]
        scaled = row * (1.0 / row[:, k : k + 1])
        column = jnp.where(below > k, both[:, k : k + 1], 0.0)
        both = both - column * scaled
    pivots = jnp.sum(both[:, :rank] * unit, axis=1, keepdims=True)
    return both[:, rank:] * (1.0 / jnp.sqrt(pivots))


def chain_kernel(
    dp, mp, a_ref, g_ref, st_ref, e_hbm, basis_ref, sketch_ref, out_hbm,
    e_ref, s_ref, es, gs, lf, lr, la, gm, ht, rt, rb, rc, rd, ro, qb, qr, nm,
    e_sem, mp_send, mp_recv, dp_send, dp_recv, pair_send, pair_recv, far_send, far_recv,
    gq, own_send, own_recv, y_send, y_recv, relay_send, relay_recv, out_sem,
):
    me_d, me_m = lax.axis_index("dp"), lax.axis_index("mp")
    rows, width = e_ref.shape
    rank = st_ref.shape[0]
    columns = g_ref.shape[1]
    slab = rows // dp
    band = rank // mp
    block = width // dp

    def load(index):
        part = pl.ds(pl.multiple_of(index * slab, slab), slab)
        return pltpu.make_async_copy(e_hbm.at[0, part], e_ref.at[part], e_sem.at[index])

    for index in range(dp):
        load(index).start()

    barrier = pltpu.get_barrier_semaphore()
    for step in range(1, mp):
        pl.semaphore_signal(
            barrier, inc=1, device_id={"mp": lax.rem(me_m + step, mp)}, device_id_type=MESH
        )
    for step in range(1, dp):
        pl.semaphore_signal(
            barrier, inc=1, device_id={"dp": lax.rem(me_d + step, dp)}, device_id_type=MESH
        )
    pl.semaphore_wait(barrier, mp + dp - 2)

    s_ref[...] = st_ref[...].T

    mine = pl.ds(pl.multiple_of(me_m * columns, columns), columns)
    gs[me_m] = jnp.dot(g_ref[...], s_ref[mine, :], preferred_element_type=F32).T.astype(BF16)
    share = Exchange(
        "mp", mp, me_m, lambda p: gs.at[me_m], lambda p: gs.at[p], mp_send.at[0], mp_recv.at[0]
    ).start()

    core, chip, chips = lax.rem(me_m, 2), me_m // 2, mp // 2
    partner = me_m + 1 - 2 * core
    deep = g_ref.shape[0] // CHUNKS

    def to_partner(source, slot, part, send_sem, recv_sem):
        return pltpu.make_async_remote_copy(
            src_ref=source.at[part],
            dst_ref=gq.at[slot, part],
            send_sem=send_sem,
            recv_sem=recv_sem,
            device_id={"mp": partner},
            device_id_type=MESH,
        )

    everything = pl.ds(0, g_ref.shape[0])
    own = to_partner(g_ref, me_m, everything, own_send.at[0], own_recv.at[0])
    own.start()
    kept = pltpu.make_async_copy(g_ref, out_hbm.at[me_m], out_sem.at[me_m])
    kept.start()
    chunk_parts = [pl.ds(c * deep, deep) for c in range(CHUNKS)]
    chunks = [
        Far(
            chips, chip, core,
            lambda p, part=part: g_ref.at[part],
            lambda p, part=part: gq.at[2 * p + core, part],
            y_send.at[c], y_recv.at[c],
        )
        for c, part in enumerate(chunk_parts)
    ]
    relayed = []

    def relay(first, last):
        for c in range(first, last):
            for hop in range(1, chips):
                chunks[c].copy(hop, False).wait_recv()
                slot = 2 * lax.rem(chip + hop, chips) + core
                relayed.append(
                    to_partner(
                        gq.at[slot], slot, chunk_parts[c],
                        relay_send.at[c, hop], relay_recv.at[c, hop],
                    )
                )
                relayed[-1].start()

    for c in range(CHUNKS // 2):
        chunks[c].start()

    def sketch_slab(index, carry):
        load(index).wait()
        part = pl.ds(pl.multiple_of(index * slab, slab), slab)
        es[part, :] = jnp.dot(e_ref[part, :], s_ref[...], preferred_element_type=F32)
        return carry

    lax.fori_loop(0, dp, sketch_slab, 0)
    share.wait()
    grad_left = jnp.dot(total(gs, mp).astype(BF16), a_ref[...], preferred_element_type=F32).T
    local_left = es[...] + grad_left
    half = slab // 2
    for index in range(dp):
        top = local_left[index * slab : index * slab + half]
        low = local_left[index * slab + half : (index + 1) * slab]
        lf[index] = jnp.concatenate([top, low], axis=1)

    share = Exchange(
        "dp", dp, me_d, lambda p: lf.at[p], lambda p: lr.at[p], dp_send.at[0], dp_recv.at[0]
    ).start()
    lr[me_d] = lf[me_d]
    share.wait()
    la[me_d] = total(lr, dp)
    share = Exchange(
        "dp", dp, me_d, lambda p: la.at[me_d], lambda p: la.at[p], dp_send.at[1], dp_recv.at[1]
    ).start()
    share.wait()
    left = jnp.concatenate(
        [la[i][:, j * rank : (j + 1) * rank] for i in range(dp) for j in range(2)], axis=0
    )
    gm[me_m] = jnp.dot(left.T, left, precision=HIGHEST, preferred_element_type=F32)
    share = Exchange(
        "mp", mp, me_m, lambda p: gm.at[me_m], lambda p: gm.at[p], mp_send.at[1], mp_recv.at[1]
    ).start()
    share.wait()
    mid = CHUNKS // 2
    chunks[mid].start()
    relay(0, mid)
    inverse = inverse_factor(total(gm, mp))
    basis = jnp.dot(left, inverse.T, precision=HIGHEST, preferred_element_type=F32)
    basis_ref[...] = basis.astype(BF16)
    basis_t = basis.T.astype(BF16)

    ht[me_m] = jnp.dot(a_ref[...], basis_ref[...], preferred_element_type=F32).T.astype(BF16)
    share = Exchange(
        "mp", mp, me_m, lambda p: ht.at[me_m], lambda p: ht.at[p], mp_send.at[2], mp_recv.at[2]
    ).start()
    chunks[mid + 1].start()

    def right_block(index, carry):
        part = pl.ds(pl.multiple_of(index * block, block), block)
        rt[:, part] = jnp.dot(basis_t, e_ref[:, part], preferred_element_type=F32)
        return carry

    lax.fori_loop(0, dp, right_block, 0)
    share.wait()
    rt[:, mine] = rt[:, mine] + jnp.dot(
        total(ht, mp).astype(BF16), g_ref[...], preferred_element_type=F32
    )

    def pair_copy(sem, d, source, target):
        return pltpu.make_async_remote_copy(
            src_ref=source,
            dst_ref=target,
            send_sem=pair_send.at[sem, d],
            recv_sem=pair_recv.at[sem, d],
            device_id={"mp": partner},
            device_id_type=MESH,
        )

    def far(sem, d, source, target):
        return Far(chips, chip, core, source, target, far_send.at[sem, d], far_recv.at[sem, d])

    pairs, fars = [], []
    for d in range(dp):
        for m in range(mp):
            rb[d, m % 2, m // 2] = rt[
                m * band : (m + 1) * band, d * block : (d + 1) * block
            ].astype(BF16)
        pairs.append(pair_copy(0, d, rb.at[d, 1 - core], rc.at[d]))
        pairs[-1].start()
    for d in range(dp):
        pairs[d].wait_recv()
        rd[d] = (rb[d, core].astype(F32) + rc[d].astype(F32)).astype(BF16)
        fars.append(far(0, d, lambda p, d=d: rd.at[d, p], lambda p, d=d: ro.at[d, p]))
        fars[-1].start()
        ro[d, chip] = rd[d, chip]
    for c in range(mid + 2, CHUNKS):
        chunks[c].start()
    relay(mid, mid + 2)
    for d in range(dp):
        fars[d].wait_recv()
        qb[d] = total(ro.at[d], chips).astype(BF16)

        @pl.when(me_d != d)
        def _():
            pltpu.make_async_remote_copy(
                src_ref=qb.at[d],
                dst_ref=qr.at[me_d],
                send_sem=dp_send.at[2, d],
                recv_sem=dp_recv.at[2, me_d],
                device_id={"dp": d},
                device_id_type=MESH,
            ).start()

    for each in pairs + fars:
        each.wait_send()
    qr[me_d] = qb[me_d]
    for step in range(1, dp):
        peer = lax.rem(me_d + step, dp)
        pltpu.make_async_remote_copy(
            src_ref=qb.at[peer],
            dst_ref=qr.at[peer],
            send_sem=dp_send.at[2, peer],
            recv_sem=dp_recv.at[2, peer],
            device_id={"dp": peer},
            device_id_type=MESH,
        ).wait()

    nm[me_m, me_d] = total(qr, dp).astype(BF16)
    share = Exchange(
        "dp", dp, me_d, lambda p: nm.at[me_m, me_d], lambda p: nm.at[me_m, p],
        dp_send.at[3], dp_recv.at[3],
    ).start()
    pairs, fars = [], []
    for step in range(dp):
        d = lax.rem(me_d + step, dp)
        if step:
            share.copy(step, False).wait_recv()
        fars.append(
            far(
                1, step,
                lambda p, d=d: nm.at[me_m, d],
                lambda p, d=d: nm.at[2 * p + core, d],
            ).start()
        )
        pairs.append(pair_copy(1, step, nm.at[me_m, d], nm.at[me_m, d]))
        pairs[-1].start()
    relay(mid + 2, CHUNKS)
    own.wait()
    for each in chunks:
        each.wait_send()
    for copy in relayed:
        copy.wait()
    for hop in range(1, mp):
        slot = lax.rem(me_m + hop, mp)
        pltpu.make_async_copy(gq.at[slot], out_hbm.at[slot], out_sem.at[slot]).start()
    relays = []
    for step in range(dp):
        d = lax.rem(me_d + step, dp)
        for hop in range(1, chips):
            fars[step].copy(hop, False).wait_recv()
            slot = 2 * lax.rem(chip + hop, chips) + core
            relays.append(pair_copy(1 + hop, step, nm.at[slot, d], nm.at[slot, d]))
            relays[-1].start()
    for copy in pairs + relays:
        copy.wait()
    for each in fars:
        each.wait_send()
    share.wait_send()
    for hop in range(1, mp):
        slot = lax.rem(me_m + hop, mp)
        pltpu.make_async_copy(gq.at[slot], out_hbm.at[slot], out_sem.at[slot]).wait()
    kept.wait()
    for m in range(mp):
        for d in range(dp):
            sketch_ref[m * band : (m + 1) * band, d * block : (d + 1) * block] = nm[m, d]


def finish_kernel(dp, a_ref, g_ref, e_ref, n_ref, b_ref, m_ref, error_ref, momentum_ref, turned):
    index = pl.program_id(0)

    @pl.when(index == 0)
    def _():
        turned[...] = a_ref[...].T

    product = jnp.dot(turned[...], g_ref[0], preferred_element_type=F32)
    fed = (product + e_ref[0].astype(F32)).astype(BF16)
    decoded = jnp.dot(b_ref[...], n_ref[...], preferred_element_type=F32)
    error_ref[0] = (fed.astype(F32) - decoded / dp).astype(BF16)

    @pl.when(index == lax.axis_index("dp"))
    def _():
        momentum_ref[...] = beta_decay * m_ref[...] + decoded


def step(dp, mp, activations, out_grads, error, sketch, momentum):
    tokens, rows = activations.shape
    columns = out_grads.shape[1]
    width, rank = sketch.shape
    block = momentum.shape[1]
    if rows % (16 * dp) or rank % (16 * mp) or block % 128 or columns % block or mp % 2 or tokens % (16 * CHUNKS):
        return native(activations, out_grads, error, sketch, momentum)
    slab, band = rows // dp, rank // mp
    vmem = pl.BlockSpec(memory_space=pltpu.VMEM)
    basis, sketch_t, gathered = pl.pallas_call(
        functools.partial(chain_kernel, dp, mp),
        out_shape=(
            jax.ShapeDtypeStruct((rows, rank), BF16),
            jax.ShapeDtypeStruct((rank, width), BF16),
            jax.ShapeDtypeStruct((mp, tokens, columns), BF16),
        ),
        in_specs=[vmem, vmem, vmem, pl.BlockSpec(memory_space=pl.ANY)],
        out_specs=(vmem, vmem, pl.BlockSpec(memory_space=pl.ANY)),
        scratch_shapes=[
            pltpu.VMEM((rows, width), BF16),
            pltpu.VMEM((width, rank), BF16),
            pltpu.VMEM((rows, rank), F32),
            pltpu.VMEM((mp, rank, tokens), BF16),
            pltpu.VMEM((dp, slab // 2, 2 * rank), F32),
            pltpu.VMEM((dp, slab // 2, 2 * rank), F32),
            pltpu.VMEM((dp, slab // 2, 2 * rank), F32),
            pltpu.VMEM((mp, rank, rank), F32),
            pltpu.VMEM((mp, rank, tokens), BF16),
            pltpu.VMEM((rank, width), F32),
            pltpu.VMEM((dp, 2, mp // 2, band, block), BF16),
            pltpu.VMEM((dp, mp // 2, band, block), BF16),
            pltpu.VMEM((dp, mp // 2, band, block), BF16),
            pltpu.VMEM((dp, mp // 2, band, block), BF16),
            pltpu.VMEM((dp, band, block), BF16),
            pltpu.VMEM((dp, band, block), BF16),
            pltpu.VMEM((mp, dp, band, block), BF16),
            pltpu.SemaphoreType.DMA((dp,)),
            pltpu.SemaphoreType.DMA((5, mp)),
            pltpu.SemaphoreType.DMA((5, mp)),
            pltpu.SemaphoreType.DMA((4, dp)),
            pltpu.SemaphoreType.DMA((4, dp)),
            pltpu.SemaphoreType.DMA((1 + mp // 2, dp)),
            pltpu.SemaphoreType.DMA((1 + mp // 2, dp)),
            pltpu.SemaphoreType.DMA((2, dp, mp // 2)),
            pltpu.SemaphoreType.DMA((2, dp, mp // 2)),
            pltpu.VMEM((mp, tokens, columns), BF16),
            pltpu.SemaphoreType.DMA((1,)),
            pltpu.SemaphoreType.DMA((1,)),
            pltpu.SemaphoreType.DMA((CHUNKS, mp // 2)),
            pltpu.SemaphoreType.DMA((CHUNKS, mp // 2)),
            pltpu.SemaphoreType.DMA((CHUNKS, mp // 2)),
            pltpu.SemaphoreType.DMA((CHUNKS, mp // 2)),
            pltpu.SemaphoreType.DMA((mp,)),
        ],
        compiler_params=pltpu.CompilerParams(
            collective_id=0, has_side_effects=True, vmem_limit_bytes=56 << 20
        ),
        cost_estimate=pl.CostEstimate(
            flops=4 * rows * width * rank, bytes_accessed=8 * rows * width, transcendentals=0
        ),
        name="chain",
    )(activations, out_grads, sketch.T, error)
    per = columns // block
    whole = lambda shape: pl.BlockSpec(shape, lambda i: (0,) * len(shape))
    error_new, momentum_new = pl.pallas_call(
        functools.partial(finish_kernel, dp),
        grid=(dp,),
        out_shape=(
            jax.ShapeDtypeStruct(error.shape, BF16),
            jax.ShapeDtypeStruct(momentum.shape, F32),
        ),
        in_specs=[
            whole((tokens, rows)),
            pl.BlockSpec((1, tokens, block), lambda i: (i // per, 0, i % per)),
            pl.BlockSpec((1, rows, block), lambda i: (0, 0, i)),
            pl.BlockSpec((rank, block), lambda i: (0, i)),
            whole((rows, rank)),
            whole((rows, block)),
        ],
        out_specs=(
            pl.BlockSpec((1, rows, block), lambda i: (0, 0, i)),
            whole((rows, block)),
        ),
        scratch_shapes=[pltpu.VMEM((rows, tokens), BF16)],
        compiler_params=pltpu.CompilerParams(
            dimension_semantics=("arbitrary",), vmem_limit_bytes=56 << 20
        ),
        name="finish",
    )(activations, gathered, error, sketch_t, basis, momentum)
    return (error_new, momentum_new, sketch_t.T)


def solution(mesh):
    body = functools.partial(step, mesh.shape["dp"], mesh.shape["mp"])
    in_specs = (P("dp", "mp"), P("dp", "mp"), P("dp", "mp", None), P(), P("mp", "dp"))
    out_specs = (P("dp", "mp", None), P("mp", "dp"), P())
    return jax.shard_map(body, mesh=mesh, in_specs=in_specs, out_specs=out_specs, check_vma=False)
```
